1024 devices in a mesh: clip: 32 (over y_hi, x), seq: 16 (over y_lo, z), tp: 2 (over core).
Axes of the slice: x: 8, y: 8 (y_hi: 4, y_lo: 2; y = y_hi * 2 + y_lo), z: 8, core: 2. Of those that a mesh axis runs over, the one named last changes fastest.
Arguments:
- ffn_hidden: bfloat16 [4096, 10240], P('clip', 'tp'), may hold values from -6 to 6
- ffn_weight: bfloat16 [10240, 4096], P('tp', 'seq'), may hold values from -0.0625 to 0.0625
- residual: bfloat16 [4096, 4096], P('clip', 'seq'), may hold values from -6 to 6
- norm_gain: float32 [4096], replicated, may hold values from 0.3 to 3
- kv_weight: bfloat16 [4096, 32, 256], P(None, ('seq', 'tp')), may hold values from -0.09375 to 0.09375
- destination: int32 [4096, 1], replicated, may hold values from 0 to 31; in each aligned block of 128 rows (0 to 127, 128 to 255, ...) at most 16 rows name the same one
- queries: bfloat16 [131072, 4096], P(('clip', 'seq', 'tp')), may hold values from -360 to 360
Outputs:
- attended: bfloat16 [131072, 4096], P(('clip', 'seq', 'tp'))
The draws below stay inside these ranges and needn't reach their ends.
Inputs may be any that keep to these rules, and one draw needn't show every extreme that they name: `destination`: in each aligned block of 128 rows no clip is named by more than 16 rows, a bound that some block reaches; every clip is named by some row.
All inputs are finite; a program needn't handle non-finite values.
Results may differ from the reference program's by a relative error of at most 0.01375.
The reference program's roundings to bfloat16 on the way (of `text`, `normed`, `keyval` and `probs`) count: a program that leaves them out, or rounds other values in their place, can miss the bound.
Values may be sent and summed in bfloat16 or wider, within the bound.
A program may use at most 64 MiB of HBM per device.

```python
import math
import jax
import jax.numpy as jnp
import numpy as np
from jax import lax

D_TEXT = 4096
FF = 10240
HEAD_DIM = 128
ROWS_CLIP = 128
HEADS = 32
QW = 4096
CAP = 16
SLOTS = 512
TOTAL_ROWS = 4096
VIDEO = 4096
TOKENS = 131072
N_CLIP = 32


def draw_queries(key, part):
    first = jax.random.fold_in(key, 11)
    base = 1.5 * jax.random.truncated_normal(first, -6.0, 6.0, (TOKENS, QW), jnp.float32)
    return base.astype(jnp.bfloat16)


def block_levels(key, extent, cuts, least, top_value):
    gain, own = 1.0, jax.random.fold_in(key, 6)
    for position, shards_of in cuts:
        steps = jnp.exp(jax.random.uniform(jax.random.fold_in(own, position), (shards_of,), jnp.float32, least / len(cuts), top_value / len(cuts)))
        gain = gain * jnp.repeat(steps, extent[position] // shards_of).reshape([-1 if axis == position else 1 for axis in range(len(extent))])
    return gain


def shared_out(own_key, own, number, rows, amount, top, limit, skew):
    order = jax.random.permutation(own_key, amount)
    crowded, common = portions_of(amount, rows * top, limit, skew, True), portions_of(amount, rows * top, limit, skew, False)
    places = jnp.arange(amount)

    def named(sizes, rotation):
        used = int((sizes > 0).sum())
        fixed = max(1, used // 4)
        passed = fixed + (places - fixed + rotation * (used - fixed)) % max(1, amount - fixed)
        return jnp.zeros((amount,), jnp.int32).at[order[jnp.where(places < fixed, places, passed)]].set(jnp.asarray(sizes, jnp.int32))

    sizes = jnp.where(number % 4 == 0, named(crowded, number // 4), named(common, number - number // 4 - 1))
    mixed = jax.random.permutation(jax.random.fold_in(own, 3), amount)
    source_of, sink = mixed[0:amount // 2 * 2:2], mixed[1:amount // 2 * 2:2]
    room = jnp.minimum(sizes[source_of] - 1, limit - sizes[sink]) // 2
    room = jnp.where((source_of == order[0]) | (sink == order[0]) | (sizes[sink] == 0), 0, jnp.maximum(room, 0))
    passed = jax.random.randint(jax.random.fold_in(own, 4), (amount // 2,), 0, 1 << 20) % (room + 1)
    sizes = sizes.at[source_of].add(-passed).at[sink].add(passed)
    labels = jnp.searchsorted(jnp.cumsum(sizes), jnp.arange(rows * top), side="right").astype(jnp.int32)
    listing = labels.reshape(top, rows).T
    listing = listing[jax.random.permutation(jax.random.fold_in(own, 1), rows)]
    rotation = jax.random.randint(jax.random.fold_in(own, 2), (rows, 1), 0, top)
    return jnp.take_along_axis(listing, (jnp.arange(top)[None, :] + rotation) % top, axis=1)


def portions_of(number_of, total, limit, slope, full):
    loads = [(1 << 20) // math.isqrt(grade ** slope) + 1 for grade in range(1, number_of + 1)]
    largest = limit if full else min(limit, max(-(-total // number_of), total * loads[0] // sum(loads)))
    least = 1 if total - largest >= number_of - 1 else 0
    counts, spare = [largest] + [least] * (number_of - 1), total - largest - least * (number_of - 1)
    while spare > 0:
        movable = [i for i in range(1, number_of) if counts[i] < largest] or [i for i in range(1, number_of) if counts[i] < limit]
        pool, left = sum([loads[i] for i in movable]), spare
        for i in movable:
            more = min(limit - counts[i], max(1, left * loads[i] // pool), spare)
            counts[i] = counts[i] + more
            spare = spare - more
    return np.array(counts)


def bell_draw(own_key, shape, scale, reach, cuts=(), kind=jnp.bfloat16):
    level = block_levels(own_key, shape, cuts, -0.22, 0.18) if cuts else 1.0
    values = jax.random.normal(own_key, shape, jnp.float32) * scale * level
    return jnp.minimum(jnp.maximum(values, -reach), reach).astype(kind)


def setup_inputs(seed: int = 0) -> dict:
    arg_keys = jax.random.split(jax.random.key(seed), 8)
    ffn_hidden = bell_draw(arg_keys[0], (TOTAL_ROWS, FF), 1.0, 6.0, ((0, 32), (1, 2)))
    ffn_weight = bell_draw(arg_keys[1], (FF, D_TEXT), FF ** -0.5, 0.0625, ((0, 2), (1, 16)))
    residual = bell_draw(arg_keys[2], (TOTAL_ROWS, D_TEXT), 1.0, 6.0, ((0, 32), (1, 16)))
    norm_gain = jnp.clip(jnp.exp(jax.random.uniform(arg_keys[3], (D_TEXT,), jnp.float32, math.log(0.3), math.log(3.0))), 0.3, 3.0)
    kv_weight = bell_draw(arg_keys[4], (D_TEXT, HEADS, 2 * HEAD_DIM), D_TEXT ** -0.5, 0.09375, ((1, 32),))
    destination_keys = jax.random.split(jax.random.fold_in(arg_keys[5], 1), TOTAL_ROWS // ROWS_CLIP)
    destination_turns = jax.random.permutation(jax.random.fold_in(arg_keys[5], 3), TOTAL_ROWS // ROWS_CLIP)
    destination = jax.vmap(lambda own, number: shared_out(jax.random.fold_in(arg_keys[5], 2), own, number, ROWS_CLIP, N_CLIP, 1, CAP, 2))(destination_keys, destination_turns).reshape((TOTAL_ROWS, 1))
    queries = draw_queries(jax.random.fold_in(arg_keys[7], 71), 0)
    return {"ffn_hidden": ffn_hidden, "ffn_weight": ffn_weight, "residual": residual, "norm_gain": norm_gain, "kv_weight": kv_weight, "destination": destination, "queries": queries}


def attend_ref(query, keyval, valid):
    keys = keyval[:, :, :HEAD_DIM].astype(jnp.float32)
    values = keyval[:, :, HEAD_DIM:].astype(jnp.float32)
    scores = jnp.einsum('rhd,shd->hrs', query.astype(jnp.float32), keys) / math.sqrt(HEAD_DIM)
    scores = jnp.where(valid[None, None, :], scores, -1e+30)
    peak = lax.optimization_barrier(jnp.max(scores, axis=2, keepdims=True))
    weights = jnp.where(valid[None, None, :], jnp.exp(scores - peak), 0.0)
    probs = (weights / lax.optimization_barrier(jnp.sum(weights, axis=2, keepdims=True))).astype(jnp.bfloat16)
    return jnp.einsum('hrs,shd->rhd', probs.astype(jnp.float32), values).astype(jnp.bfloat16)

def reference(ffn_hidden, ffn_weight, residual, norm_gain, kv_weight, destination, queries):
    ffn_out = jnp.dot(ffn_hidden, ffn_weight, preferred_element_type=jnp.float32)
    text = (residual.astype(jnp.float32) + ffn_out).astype(jnp.bfloat16)
    wide = text.astype(jnp.float32)
    scale = 1.0 / jnp.sqrt(lax.optimization_barrier(jnp.mean(wide * wide, axis=1, keepdims=True)) + 1e-06)
    normed = (wide * scale * norm_gain[None, :]).astype(jnp.bfloat16)
    keyval = jnp.dot(normed, kv_weight.reshape(D_TEXT, HEADS * 2 * HEAD_DIM), preferred_element_type=jnp.float32)
    keyval = keyval.astype(jnp.bfloat16).reshape(TOTAL_ROWS, HEADS, 2 * HEAD_DIM)
    dest = destination[:, 0]
    clip_ids = jnp.arange(N_CLIP, dtype=jnp.int32)
    query_clips = queries.reshape(N_CLIP, VIDEO, HEADS, HEAD_DIM)

    def one_clip(pair):
        clip, query = pair
        member = dest == clip
        chosen = jnp.nonzero(member, size=SLOTS, fill_value=0)[0].astype(jnp.int32)
        count = jnp.sum(member.astype(jnp.int32))
        valid = jnp.arange(SLOTS, dtype=jnp.int32) < count
        return attend_ref(query, keyval[chosen], valid)
    result = lax.map(one_clip, (clip_ids, query_clips))
    return result.reshape(TOKENS, QW)
```

```python
import math

import jax
import jax.numpy as jnp
from jax import lax
from jax.experimental import pallas as pl
from jax.experimental.pallas import tpu as pltpu
from jax.sharding import PartitionSpec as P

EPSILON = 1e-06
MESH = pl.DeviceIdType.MESH
F32 = jnp.float32
BF16 = jnp.bfloat16
CAPACITY = 16
ZS = 8


def remote(src, dst, send_sem, recv_sem, device):
    return pltpu.make_async_remote_copy(
        src_ref=src,
        dst_ref=dst,
        send_sem=send_sem,
        recv_sem=recv_sem,
        device_id=device,
        device_id_type=MESH,
    )


def ring_step(k):
    return 4 + (1 - 2 * (k % 2)) * ((k + 1) // 2)


def kernel(
    hid,
    wt,
    res,
    gain,
    kvw,
    dest,
    qry,
    out,
    hid_v,
    wt_v,
    res_v,
    gain_v,
    w2_v,
    dest_v,
    sel_v,
    bias_v,
    part,
    part_in,
    tbuf,
    nbuf,
    kv_out,
    kv_rows,
    packed,
    kvbuf,
    kt_v,
    qbuf,
    rbuf,
    ld,
    tp_s,
    tp_r,
    w_s,
    w_r,
    ag_s,
    ag_r,
    q_s,
    q_r,
    kx_s,
    kx_r,
    c_s,
    c_r,
    r_s,
    r_r,
):
    clips = lax.axis_size("clip")
    group = lax.axis_size("seq") * 2
    c, s, t = lax.axis_index("clip"), lax.axis_index("seq"), lax.axis_index("tp")
    y, z = s // ZS, s % ZS
    me = s * 2 + t
    other = 1 - t
    partner = (c, s, other)
    rows = hid_v.shape[0]
    half = rows // 2
    feat = part.shape[1]
    blocks = tbuf.shape[0]
    hd = 128

    barrier = pltpu.get_barrier_semaphore()

    @pl.loop(1, group)
    def _(o):
        g = (me + o) % group
        pl.semaphore_signal(barrier, inc=1, device_id=(c, g // 2, g % 2), device_id_type=MESH)

    @pl.loop(1, clips)
    def _(o):
        pl.semaphore_signal(barrier, inc=1, device_id=((c + o) % clips, s, t), device_id_type=MESH)

    def column(j):
        return pl.ds(pl.multiple_of(j * hd, hd), hd)

    def block_rows(j, size):
        return pl.ds(pl.multiple_of(j * size, size), size)

    loads = [
        pltpu.make_async_copy(dest, dest_v, ld.at[0]),
        pltpu.make_async_copy(hid, hid_v, ld.at[1]),
        pltpu.make_async_copy(wt, wt_v, ld.at[2]),
        pltpu.make_async_copy(res, res_v, ld.at[3]),
        pltpu.make_async_copy(gain, gain_v, ld.at[4]),
        pltpu.make_async_copy(kvw, w2_v.at[t], ld.at[5]),
        pltpu.make_async_copy(qry.at[:, column(me)], qbuf.at[block_rows(me, rows)], ld.at[6]),
    ]
    for load in loads:
        load.start()

    loads[0].wait()
    dest_row = dest_v[pl.ds(c, 1), :]
    clip_ids = lax.broadcasted_iota(jnp.int32, (clips, rows), 0)
    onehot = jnp.where(clip_ids == dest_row, 1.0, 0.0)
    earlier = jnp.where(
        lax.broadcasted_iota(jnp.int32, (rows, rows), 0)
        < lax.broadcasted_iota(jnp.int32, (rows, rows), 1),
        1.0,
        0.0,
    ).astype(BF16)
    before = jnp.dot(onehot.astype(BF16), earlier, preferred_element_type=F32)
    rank = jnp.sum(before * onehot, axis=0, keepdims=True)
    place = dest_row * CAPACITY + rank.astype(jnp.int32)
    slots = clips * CAPACITY
    target = lax.broadcasted_iota(jnp.int32, (slots, rows), 0)
    sel_v[...] = jnp.where(target == place, 1.0, 0.0).astype(BF16)
    counts = jnp.sum(jnp.where(dest_v[...] == c, 1.0, 0.0), axis=1, keepdims=True)
    slot = lax.broadcasted_iota(jnp.int32, (clips, slots), 1)
    source = lax.broadcasted_iota(jnp.int32, (clips, slots), 0)
    in_block = jnp.where(slot // CAPACITY == source, counts, 0.0)
    filled = jnp.sum(in_block, axis=0, keepdims=True)
    position = (lax.broadcasted_iota(jnp.int32, (1, slots), 1) % CAPACITY).astype(F32)
    bias_v[...] = jnp.where(position < filled, 0.0, -1e30)

    loads[1].wait()
    loads[2].wait()
    step = 1024
    part[...] = jnp.zeros_like(part)

    @pl.loop(0, hid_v.shape[1] // step)
    def _(k):
        at = pl.ds(pl.multiple_of(k * step, step), step)
        part[...] += jnp.dot(hid_v[:, at], wt_v[at, :], preferred_element_type=F32)

    pl.semaphore_wait(barrier, group - 1 + clips - 1)

    tp_copy = remote(part.at[block_rows(other, half)], part_in, tp_s, tp_r, partner)
    tp_copy.start()
    loads[3].wait()
    loads[4].wait()
    tp_copy.wait_recv()
    mine = part[block_rows(t, half), :] + part_in[...]
    text = res_v[block_rows(t, half), :].astype(F32) + mine
    tbuf[s] = text.astype(BF16)

    def text_copy(block, device):
        return remote(tbuf.at[block], tbuf.at[block], ag_s, ag_r.at[block], device)

    across = (1 - y) * ZS + z

    @pl.loop(0, ZS - 1)
    def _(k):
        text_copy(s, (c, y * ZS + (z + ring_step(k)) % ZS, t)).start()

    text_copy(s, (c, across, t)).start()

    def query_copy(k, dy, flip):
        peer_s = ((y + dy) % 2) * ZS + (z + ring_step(k)) % ZS
        peer_t = (t + 1 + flip) % 2
        peer = peer_s * 2 + peer_t
        return remote(
            qry.at[:, column(peer)],
            qbuf.at[block_rows(me, rows)],
            q_s,
            q_r,
            (c, peer_s, peer_t),
        )

    @pl.loop(0, 2 * ZS - 1)
    def _(i):
        query_copy(i // 2, 0, i % 2).start()

    weights = remote(kvw, w2_v.at[t], w_s, w_r, partner)
    weights.start()

    @pl.loop(0, ZS - 1)
    def _(k):
        block = y * ZS + (z + ring_step(ZS - 2 - k)) % ZS
        text_copy(block, (c, across, t)).wait_recv()
        text_copy(block, (c, across, t)).start()

    @pl.loop(0, 2 * ZS)
    def _(i):
        query_copy(i // 2, 1, i % 2).start()

    @pl.loop(0, ZS)
    def _(k):
        text_copy((1 - y) * ZS + k, (c, across, t)).wait_recv()

    def squares(b, acc):
        wide = tbuf[b].astype(F32)
        return acc + wide * wide

    total = lax.fori_loop(0, blocks, squares, jnp.zeros((half, feat), F32))
    mean = jnp.sum(total, axis=1, keepdims=True) / (blocks * feat)
    scale = lax.rsqrt(mean + EPSILON)

    @pl.loop(0, blocks)
    def _(b):
        g = gain_v[:, pl.ds(pl.multiple_of(b * feat, feat), feat)]
        nbuf[b] = (tbuf[b].astype(F32) * scale * g).astype(BF16)

    def project(head):
        def add(b, acc):
            w = w2_v[head, pl.ds(pl.multiple_of(b * feat, feat), feat), :]
            return acc + jnp.dot(nbuf[b], w, preferred_element_type=F32)

        return lax.fori_loop(0, blocks, add, jnp.zeros((half, 2 * hd), F32)).astype(BF16)

    weights.wait_recv()
    kv_out[...] = project(other)
    swap = remote(kv_out, kv_rows.at[block_rows(t, half)], kx_s, kx_r, partner)
    swap.start()
    loads[5].wait()
    kv_rows[block_rows(t, half), :] = project(t)
    remote(kv_out, kv_rows.at[block_rows(other, half)], kx_s, kx_r, partner).wait_recv()

    packed[...] = jnp.dot(sel_v[...], kv_rows[...], preferred_element_type=F32).astype(BF16)

    @pl.loop(0, clips)
    def _(o):
        d = (c + clips // 2 + o) % clips

        @pl.when(d != c)
        def _():
            remote(
                packed.at[block_rows(d, CAPACITY)],
                kvbuf.at[block_rows(c, CAPACITY)],
                c_s,
                c_r,
                (d, s, t),
            ).start()

    kvbuf[block_rows(c, CAPACITY), :] = packed[block_rows(c, CAPACITY), :]

    routed = (clips - 1) * CAPACITY
    slots_in = remote(packed.at[pl.ds(0, routed)], kvbuf.at[pl.ds(0, routed)], c_s, c_r, partner)
    slots_in.wait_recv()
    kt_v[...] = kvbuf[:, :hd].T

    moved = (group - 1) * rows
    queries_in = remote(qry.at[:, pl.ds(0, (group - 1) * hd)], qbuf.at[pl.ds(0, moved)], q_s, q_r, partner)
    queries_in.wait_recv()
    loads[6].wait()

    factor = 1.0 / math.sqrt(hd)

    def pair_of(p):
        return ((y + 1 - p % 2) % 2) * ZS + (z + ring_step(p // 2)) % ZS

    def result_copy(peer_s, peer_t):
        return remote(
            rbuf.at[block_rows(peer_s * 2 + peer_t, rows)],
            out.at[:, column(me)],
            r_s,
            r_r,
            (c, peer_s, peer_t),
        )

    @pl.loop(0, group // 2)
    def _(p):
        peer_s = pair_of(p)
        q = qbuf[block_rows(peer_s, 2 * rows), :]
        scores = jnp.dot(q, kt_v[...], preferred_element_type=F32) * factor + bias_v[...]
        peak = jnp.max(scores, axis=1, keepdims=True)
        w = jnp.exp(scores - peak)
        probs = (w * (1.0 / jnp.sum(w, axis=1, keepdims=True))).astype(BF16)
        attended = jnp.dot(probs, kvbuf[:, hd:], preferred_element_type=F32)
        rbuf[block_rows(peer_s, 2 * rows), :] = attended.astype(BF16)

        @pl.when(p > 0)
        def _():
            sent = pair_of(p - 1)
            result_copy(sent, other).start()
            result_copy(sent, t).start()

    result_copy(s, other).start()
    own = pltpu.make_async_copy(rbuf.at[block_rows(me, rows)], out.at[:, column(me)], ld.at[7])
    own.start()

    tp_copy.wait_send()
    weights.wait_send()
    remote(tbuf.at[pl.ds(0, 2 * ZS - 1)], tbuf.at[pl.ds(0, 2 * ZS - 1)], ag_s, ag_r.at[s], partner).wait_send()
    queries_in.wait_send()
    swap.wait_send()
    slots_in.wait_send()
    results = remote(rbuf.at[pl.ds(0, moved)], out.at[:, pl.ds(0, (group - 1) * hd)], r_s, r_r, partner)
    results.wait_send()
    results.wait_recv()
    own.wait()


def shards(ffn_hidden, ffn_weight, residual, norm_gain, kv_weight, destination, queries):
    rows, hidden = ffn_hidden.shape
    feat = ffn_weight.shape[1]
    width = kv_weight.shape[0]
    pair = kv_weight.shape[1] * kv_weight.shape[2]
    clips = destination.shape[0] // rows
    slots = clips * CAPACITY
    tokens = queries.shape[0]
    blocks = width // feat
    group = queries.shape[1] // 128
    half = rows // 2
    dma = pltpu.SemaphoreType.DMA
    return pl.pallas_call(
        kernel,
        out_shape=jax.ShapeDtypeStruct(queries.shape, BF16),
        in_specs=[pl.BlockSpec(memory_space=pl.ANY)] * 7,
        out_specs=pl.BlockSpec(memory_space=pl.ANY),
        scratch_shapes=[
            pltpu.VMEM((rows, hidden), BF16),
            pltpu.VMEM((hidden, feat), BF16),
            pltpu.VMEM((rows, feat), BF16),
            pltpu.VMEM((1, width), F32),
            pltpu.VMEM((2, width, pair), BF16),
            pltpu.VMEM((clips, rows), jnp.int32),
            pltpu.VMEM((slots, rows), BF16),
            pltpu.VMEM((1, slots), F32),
            pltpu.VMEM((rows, feat), F32),
            pltpu.VMEM((half, feat), F32),
            pltpu.VMEM((blocks, half, feat), BF16),
            pltpu.VMEM((blocks, half, feat), BF16),
            pltpu.VMEM((half, pair), BF16),
            pltpu.VMEM((rows, pair), BF16),
            pltpu.VMEM((slots, pair), BF16),
            pltpu.VMEM((slots, pair), BF16),
            pltpu.VMEM((pair // 2, slots), BF16),
            pltpu.VMEM((group * tokens, 128), BF16),
            pltpu.VMEM((group * tokens, 128), BF16),
            dma((8,)),
            dma,
            dma,
            dma,
            dma,
            dma,
            dma((blocks,)),
            dma,
            dma,
            dma,
            dma,
            dma,
            dma,
            dma,
            dma,
        ],
        compiler_params=pltpu.CompilerParams(
            collective_id=0, has_side_effects=True, vmem_limit_bytes=56 * 1024 * 1024
        ),
    )(
        ffn_hidden,
        ffn_weight,
        residual,
        norm_gain.reshape(1, width),
        kv_weight.reshape(width, pair),
        destination.reshape(clips, rows),
        queries,
    )


def solution(mesh):
    return jax.shard_map(
        shards,
        mesh=mesh,
        in_specs=(
            P("clip", "tp"),
            P("tp", "seq"),
            P("clip", "seq"),
            P(),
            P(None, ("seq", "tp"), None),
            P(),
            P(("clip", "seq", "tp"), None),
        ),
        out_specs=P(("clip", "seq", "tp"), None),
        check_vma=False,
    )
```

```python
import math

import jax
import jax.numpy as jnp
from jax import lax
from jax.experimental import pallas as pl
from jax.experimental.pallas import tpu as pltpu
from jax.sharding import PartitionSpec as P

EPSILON = 1e-06
MESH = pl.DeviceIdType.MESH
F32 = jnp.float32
BF16 = jnp.bfloat16
CAPACITY = 16
ZS = 8
XS = 8


def remote(src, dst, send_sem, recv_sem, device):
    return pltpu.make_async_remote_copy(
        src_ref=src,
        dst_ref=dst,
        send_sem=send_sem,
        recv_sem=recv_sem,
        device_id=device,
        device_id_type=MESH,
    )


def ring_step(k):
    return 4 + (1 - 2 * (k % 2)) * ((k + 1) // 2)


def near_step(k):
    return (1 - 2 * (k % 2)) * ((k + 1) // 2)


def gray(i):
    return i + (i // 2) * (1 - 2 * (i % 2))


def kernel(
    hid,
    wt,
    res,
    gain,
    kvw,
    dest,
    qry,
    out,
    hid_v,
    wt_v,
    res_v,
    gain_v,
    w2_v,
    dest_v,
    sel_v,
    bias_v,
    part,
    part_in,
    tbuf,
    nbuf,
    kv_out,
    kv_rows,
    packed,
    kvall,
    kt_v,
    qbuf,
    rbuf,
    ld,
    tp_s,
    tp_r,
    w_s,
    w_r,
    ag_s,
    ag_r,
    q_s,
    q_r,
    kx_s,
    kx_r,
    c_s,
    c_r,
    k_s,
    k_r,
    r_s,
    r_r,
):
    clips = lax.axis_size("clip")
    c, s, t = lax.axis_index("clip"), lax.axis_index("seq"), lax.axis_index("tp")
    y, z = s // ZS, s % ZS
    yh, x = c // XS, c % XS
    parts = clips // XS
    other = 1 - t
    partner = (c, s, other)
    across = (1 - y) * ZS + z
    member = 2 * y + t
    rows = hid_v.shape[0]
    half = rows // 2
    feat = part.shape[1]
    blocks = tbuf.shape[0]
    hd = 128
    chunk = XS * CAPACITY

    barrier = pltpu.get_barrier_semaphore()

    def greet(device):
        pl.semaphore_signal(barrier, inc=1, device_id=device, device_id_type=MESH)

    @pl.loop(1, ZS)
    def _(o):
        greet((c, y * ZS + (z + o) % ZS, t))

    greet(partner)
    greet((c, across, t))
    greet((c, across, other))

    @pl.loop(1, clips)
    def _(o):
        greet(((c + o) % clips, s, t))

    def column(j):
        return pl.ds(pl.multiple_of(j * hd, hd), hd)

    def block_rows(j, size):
        return pl.ds(pl.multiple_of(j * size, size), size)

    loads = [
        pltpu.make_async_copy(dest, dest_v, ld.at[0]),
        pltpu.make_async_copy(hid, hid_v, ld.at[1]),
        pltpu.make_async_copy(wt, wt_v, ld.at[2]),
        pltpu.make_async_copy(res, res_v, ld.at[3]),
        pltpu.make_async_copy(gain, gain_v, ld.at[4]),
        pltpu.make_async_copy(kvw, w2_v.at[t], ld.at[5]),
    ]
    for load in loads:
        load.start()

    @pl.loop(0, ZS)
    def _(k):
        pltpu.make_async_copy(
            qry.at[:, column(2 * (y * ZS + k) + t)],
            qbuf.at[k, block_rows(member, rows)],
            ld.at[6],
        ).start()

    loads[0].wait()
    dest_row = dest_v[pl.ds(c, 1), :]
    clip_ids = lax.broadcasted_iota(jnp.int32, (clips, rows), 0)
    onehot = jnp.where(clip_ids == dest_row, 1.0, 0.0)
    earlier = jnp.where(
        lax.broadcasted_iota(jnp.int32, (rows, rows), 0)
        < lax.broadcasted_iota(jnp.int32, (rows, rows), 1),
        1.0,
        0.0,
    ).astype(BF16)
    before = jnp.dot(onehot.astype(BF16), earlier, preferred_element_type=F32)
    rank = jnp.sum(before * onehot, axis=0, keepdims=True)
    place = dest_row * CAPACITY + rank.astype(jnp.int32)
    slots = clips * CAPACITY
    target = lax.broadcasted_iota(jnp.int32, (slots, rows), 0)
    sel_v[...] = jnp.where(target == place, 1.0, 0.0).astype(BF16)
    counts = jnp.sum(jnp.where(dest_v[...] == c, 1.0, 0.0), axis=1, keepdims=True)
    slot = lax.broadcasted_iota(jnp.int32, (clips, slots), 1)
    source = lax.broadcasted_iota(jnp.int32, (clips, slots), 0)
    in_block = jnp.where(slot // CAPACITY == source, counts, 0.0)
    filled = jnp.sum(in_block, axis=0, keepdims=True)
    position = (lax.broadcasted_iota(jnp.int32, (1, slots), 1) % CAPACITY).astype(F32)
    bias_v[...] = jnp.where(position < filled, 0.0, -1e30)

    loads[1].wait()
    loads[2].wait()
    step = 1024
    part[...] = jnp.zeros_like(part)

    @pl.loop(0, hid_v.shape[1] // step)
    def _(k):
        at = pl.ds(pl.multiple_of(k * step, step), step)
        part[...] += jnp.dot(hid_v[:, at], wt_v[at, :], preferred_element_type=F32)

    pl.semaphore_wait(barrier, ZS - 1 + 3 + clips - 1)

    tp_copy = remote(part.at[block_rows(other, half)], part_in, tp_s, tp_r, partner)
    tp_copy.start()
    loads[3].wait()
    loads[4].wait()
    tp_copy.wait_recv()
    mine = part[block_rows(t, half), :] + part_in[...]
    text = res_v[block_rows(t, half), :].astype(F32) + mine
    tbuf[s] = text.astype(BF16)

    def text_copy(block, device):
        return remote(tbuf.at[block], tbuf.at[block], ag_s, ag_r.at[block], device)

    @pl.loop(0, ZS - 1)
    def _(k):
        text_copy(s, (c, y * ZS + (z + ring_step(k)) % ZS, t)).start()

    text_copy(s, (c, across, t)).start()

    def send_queries(k):
        at = (z + near_step(k) + ZS) % ZS
        for peer_y, peer_t in ((1 - y, t), (1 - y, other), (y, other)):
            remote(
                qry.at[:, column(2 * (peer_y * ZS + at) + peer_t)],
                qbuf.at[at, block_rows(member, rows)],
                q_s,
                q_r.at[at],
                (c, peer_y * ZS + z, peer_t),
            ).start()

    @pl.loop(0, 2)
    def _(k):
        send_queries(k)

    weights = remote(kvw, w2_v.at[t], w_s, w_r, partner)
    weights.start()

    @pl.loop(0, ZS - 1)
    def _(k):
        block = y * ZS + (z + ring_step(ZS - 2 - k)) % ZS
        text_copy(block, (c, across, t)).wait_recv()
        text_copy(block, (c, across, t)).start()

    @pl.loop(2, ZS)
    def _(k):
        send_queries(k)

    @pl.loop(0, ZS)
    def _(k):
        text_copy((1 - y) * ZS + k, (c, across, t)).wait_recv()

    def squares(b, acc):
        wide = tbuf[b].astype(F32)
        return acc + wide * wide

    total = lax.fori_loop(0, blocks, squares, jnp.zeros((half, feat), F32))
    mean = jnp.sum(total, axis=1, keepdims=True) / (blocks * feat)
    scale = lax.rsqrt(mean + EPSILON)

    @pl.loop(0, blocks)
    def _(b):
        at = pl.ds(pl.multiple_of(b * feat, feat), feat)
        nbuf[:, at] = (tbuf[b].astype(F32) * scale * gain_v[:, at]).astype(BF16)

    def project(head):
        acc = jnp.zeros((half, 2 * hd), F32)
        for k in range(blocks * feat // step):
            at = pl.ds(k * step, step)
            acc += jnp.dot(nbuf[:, at], w2_v[head, at, :], preferred_element_type=F32)
        return acc.astype(BF16)

    weights.wait_recv()
    kv_out[...] = project(other)
    swap = remote(kv_out, kv_rows.at[block_rows(t, half)], kx_s, kx_r, partner)
    swap.start()
    loads[5].wait()
    kv_rows[block_rows(t, half), :] = project(t)
    remote(kv_out, kv_rows.at[block_rows(other, half)], kx_s, kx_r, partner).wait_recv()

    @pl.loop(0, parts)
    def _(i):
        to = (yh + gray(i)) % parts
        at = block_rows(to, chunk)
        packed[at, :] = jnp.dot(sel_v[at, :], kv_rows[...], preferred_element_type=F32).astype(BF16)

        @pl.loop(0, XS)
        def _(j):
            d = to * XS + (x + XS // 2 + j) % XS

            @pl.when(d != c)
            def _():
                remote(
                    packed.at[block_rows(d, CAPACITY)],
                    kvall.at[z, block_rows(c, CAPACITY)],
                    c_s,
                    c_r.at[i],
                    (d, s, t),
                ).start()

    stay = pltpu.make_async_copy(
        packed.at[block_rows(c, CAPACITY)], kvall.at[z, block_rows(c, CAPACITY)], ld.at[7]
    )
    stay.start()
    own_queries = pltpu.make_async_copy(qbuf.at[pl.ds(0, 2)], qbuf.at[pl.ds(0, 2)], ld.at[6])
    own_queries.wait()
    stay.wait()

    factor = 1.0 / math.sqrt(hd)
    up, down = (c, y * ZS + (z + 1) % ZS, t), (c, y * ZS + (z + ZS - 1) % ZS, t)

    def chunk_copy(place, i, device):
        at = block_rows((yh - gray(i) + parts) % parts, chunk)
        piece = kvall.at[place, at]
        return remote(piece, piece, k_s, k_r.at[place * parts + i], device)

    def arrived(i, size):
        piece = kvall.at[z, pl.ds(0, size)]
        remote(packed.at[pl.ds(0, size)], piece, c_s, c_r.at[i], partner).wait_recv()

    def unit_of(n):
        e, i = n // parts - 1, n % parts
        return (z + (2 * (i // 2) - 1) * e + ZS) % ZS, i % 2

    def is_unit(n):
        return (n >= parts) & ((n < parts + 2) | (n >= 2 * parts))

    def result_copy(place, peer_y, peer_t):
        return remote(
            rbuf.at[place, block_rows(2 * peer_y + peer_t, rows)],
            out.at[:, column(2 * (y * ZS + place) + t)],
            r_s,
            r_r,
            (c, peer_y * ZS + z, peer_t),
        )

    def send_unit(n):
        place, peer_y = unit_of(n)

        @pl.when(peer_y == y)
        def _():
            result_copy(place, y, other).start()
            pltpu.make_async_copy(
                rbuf.at[place, block_rows(member, rows)],
                out.at[:, column(2 * (y * ZS + place) + t)],
                ld.at[8],
            ).start()

        @pl.when(peer_y != y)
        def _():
            result_copy(place, 1 - y, t).start()
            result_copy(place, 1 - y, other).start()

    last = parts * (ZS // 2 + 1) + 1

    @pl.loop(0, last + 1)
    def _(n):
        d, i = n // parts, n % parts
        low, high = (z - d + ZS) % ZS, (z + d) % ZS

        @pl.when(n == 0)
        def _():
            arrived(i, chunk - CAPACITY)

        @pl.when((n > 0) & (d == 0))
        def _():
            arrived(i, chunk)

        @pl.when((d > 0) & ((d < ZS // 2) | (n < last - 1)))
        def _():
            chunk_copy(low, i, up).wait_recv()

        @pl.when((d < 3) | ((d == 3) & (i < 2)))
        def _():
            chunk_copy(low, i, up).start()

        @pl.when((d > 0) & (d < ZS // 2))
        def _():
            chunk_copy(high, i, down).wait_recv()

        @pl.when((d < 3) | ((d == 3) & (i >= 2)))
        def _():
            chunk_copy(high, i, down).start()

        @pl.when(is_unit(n - 1))
        def _():
            send_unit(n - 1)

        @pl.when(is_unit(n))
        def _():
            place, peer_y = unit_of(n)

            @pl.when(i % 2 == 0)
            def _():
                into = qbuf.at[place, pl.ds(0, 3 * rows)]
                remote(into, into, q_s, q_r.at[place], partner).wait_recv()
                kt_v[...] = kvall[place, :, :hd].T

            tokens = block_rows(peer_y, 2 * rows)
            scores = jnp.dot(qbuf[place, tokens, :], kt_v[...], preferred_element_type=F32)
            scores = scores * factor + bias_v[...]
            peak = jnp.max(scores, axis=1, keepdims=True)
            w = jnp.exp(scores - peak)
            probs = (w * (1.0 / jnp.sum(w, axis=1, keepdims=True))).astype(BF16)
            attended = jnp.dot(probs, kvall[place, :, hd:], preferred_element_type=F32)
            rbuf[place, tokens, :] = attended.astype(BF16)

    tp_copy.wait_send()
    weights.wait_send()
    remote(tbuf.at[pl.ds(0, 2 * ZS - 1)], tbuf.at[pl.ds(0, 2 * ZS - 1)], ag_s, ag_r.at[s], partner).wait_send()
    swap.wait_send()
    remote(packed.at[pl.ds(0, slots - CAPACITY)], packed.at[pl.ds(0, slots - CAPACITY)], c_s, c_r.at[0], partner).wait_send()
    send_unit(last)
    most = pl.ds(0, 3 * ZS // 4)
    remote(qbuf.at[most], qbuf.at[most], q_s, q_r.at[0], partner).wait_send()
    remote(kvall.at[pl.ds(0, ZS - 1)], kvall.at[pl.ds(0, ZS - 1)], k_s, k_r.at[0], partner).wait_send()
    here = out.at[:, pl.ds(0, ZS * hd)]
    pltpu.make_async_copy(here, here, ld.at[8]).wait()
    results = remote(rbuf.at[most], out.at[:, pl.ds(0, 3 * ZS * hd)], r_s, r_r, partner)
    results.wait_send()
    results.wait_recv()


def shards(ffn_hidden, ffn_weight, residual, norm_gain, kv_weight, destination, queries):
    rows, hidden = ffn_hidden.shape
    feat = ffn_weight.shape[1]
    width = kv_weight.shape[0]
    pair = kv_weight.shape[1] * kv_weight.shape[2]
    clips = destination.shape[0] // rows
    slots = clips * CAPACITY
    tokens = queries.shape[0]
    blocks = width // feat
    half = rows // 2
    dma = pltpu.SemaphoreType.DMA
    return pl.pallas_call(
        kernel,
        out_shape=jax.ShapeDtypeStruct(queries.shape, BF16),
        in_specs=[pl.BlockSpec(memory_space=pl.ANY)] * 7,
        out_specs=pl.BlockSpec(memory_space=pl.ANY),
        scratch_shapes=[
            pltpu.VMEM((rows, hidden), BF16),
            pltpu.VMEM((hidden, feat), BF16),
            pltpu.VMEM((rows, feat), BF16),
            pltpu.VMEM((1, width), F32),
            pltpu.VMEM((2, width, pair), BF16),
            pltpu.VMEM((clips, rows), jnp.int32),
            pltpu.VMEM((slots, rows), BF16),
            pltpu.VMEM((1, slots), F32),
            pltpu.VMEM((rows, feat), F32),
            pltpu.VMEM((half, feat), F32),
            pltpu.VMEM((blocks, half, feat), BF16),
            pltpu.VMEM((half, width), BF16),
            pltpu.VMEM((half, pair), BF16),
            pltpu.VMEM((rows, pair), BF16),
            pltpu.VMEM((slots, pair), BF16),
            pltpu.VMEM((ZS, slots, pair), BF16),
            pltpu.VMEM((pair // 2, slots), BF16),
            pltpu.VMEM((ZS, 4 * tokens, 128), BF16),
            pltpu.VMEM((ZS, 4 * tokens, 128), BF16),
            dma((9,)),
            dma,
            dma,
            dma,
            dma,
            dma,
            dma((blocks,)),
            dma,
            dma((ZS,)),
            dma,
            dma,
            dma,
            dma((clips // XS,)),
            dma,
            dma((ZS * clips // XS,)),
            dma,
            dma,
        ],
        compiler_params=pltpu.CompilerParams(
            collective_id=0, has_side_effects=True, vmem_limit_bytes=56 * 1024 * 1024
        ),
    )(
        ffn_hidden,
        ffn_weight,
        residual,
        norm_gain.reshape(1, width),
        kv_weight.reshape(width, pair),
        destination.reshape(clips, rows),
        queries,
    )


def solution(mesh):
    return jax.shard_map(
        shards,
        mesh=mesh,
        in_specs=(
            P("clip", "tp"),
            P("tp", "seq"),
            P("clip", "seq"),
            P(),
            P(None, ("seq", "tp"), None),
            P(),
            P(("clip", "seq", "tp"), None),
        ),
        out_specs=P(("clip", "seq", "tp"), None),
        check_vma=False,
    )
```

```python
import math

import jax
import jax.numpy as jnp
from jax import lax
from jax.experimental import pallas as pl
from jax.experimental.pallas import tpu as pltpu
from jax.sharding import PartitionSpec as P

EPSILON = 1e-06
MESH = pl.DeviceIdType.MESH
F32 = jnp.float32
BF16 = jnp.bfloat16
CAPACITY = 16
EARLY = 1
ZS = 8
XS = 8


def remote(src, dst, send_sem, recv_sem, device):
    return pltpu.make_async_remote_copy(
        src_ref=src,
        dst_ref=dst,
        send_sem=send_sem,
        recv_sem=recv_sem,
        device_id=device,
        device_id_type=MESH,
    )


def near_step(k):
    return (1 - 2 * (k % 2)) * ((k + 1) // 2)


def gray(i):
    return i + (i // 2) * (1 - 2 * (i % 2))


def kernel(
    hid,
    wt,
    res,
    gain,
    kvw,
    dest,
    qry,
    out,
    hid_v,
    wt_v,
    res_v,
    gain_v,
    w2_v,
    dest_v,
    sel_v,
    bias_v,
    part,
    part_in,
    tbuf,
    nbuf,
    kv_out,
    kv_rows,
    packed,
    kvall,
    kt_v,
    qbuf,
    rbuf,
    ld,
    tp_s,
    tp_r,
    w_s,
    w_r,
    ag_s,
    ag_r,
    q_s,
    q_r,
    kx_s,
    kx_r,
    c_s,
    c_r,
    k_s,
    k_r,
    r_s,
    r_r,
):
    clips = lax.axis_size("clip")
    c, s, t = lax.axis_index("clip"), lax.axis_index("seq"), lax.axis_index("tp")
    y, z = s // ZS, s % ZS
    yh, x = c // XS, c % XS
    parts = clips // XS
    other = 1 - t
    partner = (c, s, other)
    across = (1 - y) * ZS + z
    member = 2 * y + t
    rows = hid_v.shape[0]
    half = rows // 2
    feat = part.shape[1]
    blocks = tbuf.shape[0]
    hd = 128
    chunk = XS * CAPACITY

    barrier = pltpu.get_barrier_semaphore()

    def greet(device):
        pl.semaphore_signal(barrier, inc=1, device_id=device, device_id_type=MESH)

    @pl.loop(0, clips)
    def _(o):
        to = (yh + 2 + o // XS) % parts * XS + (x + XS // 2 + o) % XS

        @pl.when(to != c)
        def _():
            greet((to, s, t))

    @pl.loop(1, ZS)
    def _(o):
        greet((c, y * ZS + (z + o) % ZS, t))

    greet((c, across, t))
    greet((c, across, other))
    greet(partner)

    def column(j):
        return pl.ds(pl.multiple_of(j * hd, hd), hd)

    def block_rows(j, size):
        return pl.ds(pl.multiple_of(j * size, size), size)

    step = 1024
    depths = [pl.ds(k * step, step) for k in range(hid_v.shape[1] // step)]
    loads = []
    for k, at in enumerate(depths):
        loads.append(pltpu.make_async_copy(hid.at[:, at], hid_v.at[:, at], ld.at[9 + 2 * k]))
        loads.append(pltpu.make_async_copy(wt.at[at], wt_v.at[at], ld.at[10 + 2 * k]))
    dest_load = pltpu.make_async_copy(dest, dest_v, ld.at[0])
    res_load = pltpu.make_async_copy(res, res_v, ld.at[3])
    gain_load = pltpu.make_async_copy(gain, gain_v, ld.at[4])
    w_load = pltpu.make_async_copy(kvw, w2_v.at[t], ld.at[5])
    for load in loads + [res_load, dest_load, gain_load, w_load]:
        load.start()

    @pl.loop(0, ZS)
    def _(k):
        pltpu.make_async_copy(
            qry.at[:, column(2 * (y * ZS + k) + t)],
            qbuf.at[k, block_rows(member, rows)],
            ld.at[6],
        ).start()

    total = jnp.zeros(part.shape, F32)
    for k, at in enumerate(depths):
        loads[2 * k].wait()
        loads[2 * k + 1].wait()
        total += jnp.dot(hid_v[:, at], wt_v[at, :], preferred_element_type=F32)
    part[...] = total

    pl.semaphore_wait(barrier, ZS - 1 + 3 + clips - 1)

    tp_copy = remote(part.at[block_rows(other, half)], part_in, tp_s, tp_r, partner)
    tp_copy.start()
    res_load.wait()
    tp_copy.wait_recv()
    mine = part[block_rows(t, half), :] + part_in[...]
    text = res_v[block_rows(t, half), :].astype(F32) + mine
    tbuf[s] = text.astype(BF16)

    def text_copy(block, device):
        return remote(tbuf.at[block], tbuf.at[block], ag_s, ag_r.at[block], device)

    def along(d):
        return y * ZS + (z + d + ZS) % ZS

    def pass_on(block, to):
        text_copy(block, (c, to, t)).start()

    for to in (across, along(-1), along(1), along(-2), along(2)):
        pass_on(s, to)

    def send_queries(k):
        at = (z + near_step(k) + ZS) % ZS
        for peer_y, peer_t in ((1 - y, t), (1 - y, other), (y, other)):
            remote(
                qry.at[:, column(2 * (peer_y * ZS + at) + peer_t)],
                qbuf.at[at, block_rows(member, rows)],
                q_s,
                q_r.at[at],
                (c, peer_y * ZS + z, peer_t),
            ).start()

    weights = remote(kvw, w2_v.at[t], w_s, w_r, partner)
    weights.start()

    dest_load.wait()
    dest_row = dest_v[pl.ds(c, 1), :]
    clip_ids = lax.broadcasted_iota(jnp.int32, (clips, rows), 0)
    onehot = jnp.where(clip_ids == dest_row, 1.0, 0.0)
    earlier = jnp.where(
        lax.broadcasted_iota(jnp.int32, (rows, rows), 0)
        < lax.broadcasted_iota(jnp.int32, (rows, rows), 1),
        1.0,
        0.0,
    ).astype(BF16)
    before = jnp.dot(onehot.astype(BF16), earlier, preferred_element_type=F32)
    rank = jnp.sum(before * onehot, axis=0, keepdims=True)
    place = dest_row * CAPACITY + rank.astype(jnp.int32)
    slots = clips * CAPACITY
    target = lax.broadcasted_iota(jnp.int32, (slots, rows), 0)
    sel_v[...] = jnp.where(target == place, 1.0, 0.0).astype(BF16)
    counts = jnp.sum(jnp.where(dest_v[...] == c, 1.0, 0.0), axis=1, keepdims=True)
    slot = lax.broadcasted_iota(jnp.int32, (clips, slots), 1)
    source = lax.broadcasted_iota(jnp.int32, (clips, slots), 0)
    in_block = jnp.where(slot // CAPACITY == source, counts, 0.0)
    filled = jnp.sum(in_block, axis=0, keepdims=True)
    position = (lax.broadcasted_iota(jnp.int32, (1, slots), 1) % CAPACITY).astype(F32)
    bias_v[...] = jnp.where(position < filled, 0.0, -1e30)

    for d in (-1, 1, -2, 2, -3, 3, 4):
        block = along(d)
        text_copy(block, (c, across, t)).wait_recv()
        if d in (-2, 2):
            onward = -d // 2
            pass_on(block, along(onward))

            @pl.when(t == (0 if d < 0 else 1))
            def _(block=block, onward=onward):
                pass_on(block, along(2 * onward))

        pass_on(block, across)

    @pl.loop(0, ZS)
    def _(k):
        text_copy((1 - y) * ZS + k, (c, across, t)).wait_recv()

    @pl.loop(0, EARLY)
    def _(k):
        send_queries(k)

    gain_load.wait()

    def squares(b, acc):
        wide = tbuf[b].astype(F32)
        return acc + wide * wide

    total = lax.fori_loop(0, blocks, squares, jnp.zeros((half, feat), F32))
    mean = jnp.sum(total, axis=1, keepdims=True) / (blocks * feat)
    scale = lax.rsqrt(mean + EPSILON)

    @pl.loop(0, blocks)
    def _(b):
        at = pl.ds(pl.multiple_of(b * feat, feat), feat)
        nbuf[:, at] = (tbuf[b].astype(F32) * scale * gain_v[:, at]).astype(BF16)

    def project(head):
        acc = jnp.zeros((half, 2 * hd), F32)
        for k in range(blocks * feat // step):
            at = pl.ds(k * step, step)
            acc += jnp.dot(nbuf[:, at], w2_v[head, at, :], preferred_element_type=F32)
        return acc.astype(BF16)

    weights.wait_recv()
    kv_out[...] = project(other)
    swap = remote(kv_out, kv_rows.at[block_rows(t, half)], kx_s, kx_r, partner)
    swap.start()
    w_load.wait()
    kv_rows[block_rows(t, half), :] = project(t)
    remote(kv_out, kv_rows.at[block_rows(other, half)], kx_s, kx_r, partner).wait_recv()

    @pl.loop(0, parts)
    def _(i):
        to = (yh + gray(i)) % parts
        at = block_rows(to, chunk)
        packed[at, :] = jnp.dot(sel_v[at, :], kv_rows[...], preferred_element_type=F32).astype(BF16)

        @pl.loop(0, XS)
        def _(j):
            d = to * XS + (x + XS // 2 + j) % XS

            @pl.when(d != c)
            def _():
                remote(
                    packed.at[block_rows(d, CAPACITY)],
                    kvall.at[z, block_rows(c, CAPACITY)],
                    c_s,
                    c_r.at[i],
                    (d, s, t),
                ).start()

    stay = pltpu.make_async_copy(
        packed.at[block_rows(c, CAPACITY)], kvall.at[z, block_rows(c, CAPACITY)], ld.at[7]
    )
    stay.start()
    own_queries = pltpu.make_async_copy(qbuf.at[pl.ds(0, 2)], qbuf.at[pl.ds(0, 2)], ld.at[6])
    own_queries.wait()
    stay.wait()

    factor = 1.0 / math.sqrt(hd)
    up, down = (c, y * ZS + (z + 1) % ZS, t), (c, y * ZS + (z + ZS - 1) % ZS, t)

    def chunk_copy(place, i, device):
        at = block_rows((yh - gray(i) + parts) % parts, chunk)
        piece = kvall.at[place, at]
        return remote(piece, piece, k_s, k_r.at[place * parts + i], device)

    def arrived(i, size):
        piece = kvall.at[z, pl.ds(0, size)]
        remote(packed.at[pl.ds(0, size)], piece, c_s, c_r.at[i], partner).wait_recv()

    def unit_of(n):
        e, i = n // parts - 1, n % parts
        return (z + (2 * (i // 2) - 1) * e + ZS) % ZS, (i + 1 + y) % 2

    def is_unit(n):
        return (n >= parts) & ((n < parts + 2) | (n >= 2 * parts))

    def result_copy(place, peer_y, peer_t):
        return remote(
            rbuf.at[place, block_rows(2 * peer_y + peer_t, rows)],
            out.at[:, column(2 * (y * ZS + place) + t)],
            r_s,
            r_r,
            (c, peer_y * ZS + z, peer_t),
        )

    def send_unit(n):
        place, peer_y = unit_of(n)

        @pl.when(peer_y == y)
        def _():
            result_copy(place, y, other).start()
            pltpu.make_async_copy(
                rbuf.at[place, block_rows(member, rows)],
                out.at[:, column(2 * (y * ZS + place) + t)],
                ld.at[8],
            ).start()

        @pl.when(peer_y != y)
        def _():
            result_copy(place, 1 - y, t).start()
            result_copy(place, 1 - y, other).start()

    last = parts * (ZS // 2 + 1) + 1

    @pl.loop(0, last + 1)
    def _(n):
        d, i = n // parts, n % parts
        low, high = (z - d + ZS) % ZS, (z + d) % ZS

        @pl.when(n == 0)
        def _():
            arrived(i, chunk - CAPACITY)

        @pl.when((n > 0) & (d == 0))
        def _():
            arrived(i, chunk)

        @pl.when((d > 0) & ((d < ZS // 2) | (n < last - 1)))
        def _():
            chunk_copy(low, i, up).wait_recv()

        @pl.when((d < 3) | ((d == 3) & (i < 2)))
        def _():
            chunk_copy(low, i, up).start()

        @pl.when((d > 0) & (d < ZS // 2))
        def _():
            chunk_copy(high, i, down).wait_recv()

        @pl.when((d < 3) | ((d == 3) & (i >= 2)))
        def _():
            chunk_copy(high, i, down).start()

        @pl.when((n >= parts - 1) & (n < parts - 1 + ZS - EARLY))
        def _():
            send_queries(n - parts + 1 + EARLY)

        @pl.when(is_unit(n - 1))
        def _():
            send_unit(n - 1)

        @pl.when(is_unit(n))
        def _():
            place, peer_y = unit_of(n)

            @pl.when(i % 2 == 0)
            def _():
                into = qbuf.at[place, pl.ds(0, 3 * rows)]
                remote(into, into, q_s, q_r.at[place], partner).wait_recv()
                kt_v[...] = kvall[place, :, :hd].T

            tokens = block_rows(peer_y, 2 * rows)
            scores = jnp.dot(qbuf[place, tokens, :], kt_v[...], preferred_element_type=F32)
            scores = scores * factor + bias_v[...]
            peak = jnp.max(scores, axis=1, keepdims=True)
            w = jnp.exp(scores - peak)
            probs = (w * (1.0 / jnp.sum(w, axis=1, keepdims=True))).astype(BF16)
            attended = jnp.dot(probs, kvall[place, :, hd:], preferred_element_type=F32)
            rbuf[place, tokens, :] = attended.astype(BF16)

    tp_copy.wait_send()
    weights.wait_send()
    remote(tbuf.at[pl.ds(0, 2 * ZS - 1)], tbuf.at[pl.ds(0, 2 * ZS - 1)], ag_s, ag_r.at[s], partner).wait_send()
    swap.wait_send()
    remote(packed.at[pl.ds(0, slots - CAPACITY)], packed.at[pl.ds(0, slots - CAPACITY)], c_s, c_r.at[0], partner).wait_send()
    send_unit(last)
    most = pl.ds(0, 3 * ZS // 4)
    remote(qbuf.at[most], qbuf.at[most], q_s, q_r.at[0], partner).wait_send()
    remote(kvall.at[pl.ds(0, ZS - 1)], kvall.at[pl.ds(0, ZS - 1)], k_s, k_r.at[0], partner).wait_send()
    here = out.at[:, pl.ds(0, ZS * hd)]
    pltpu.make_async_copy(here, here, ld.at[8]).wait()
    results = remote(rbuf.at[most], out.at[:, pl.ds(0, 3 * ZS * hd)], r_s, r_r, partner)
    results.wait_send()
    results.wait_recv()


def shards(ffn_hidden, ffn_weight, residual, norm_gain, kv_weight, destination, queries):
    rows, hidden = ffn_hidden.shape
    feat = ffn_weight.shape[1]
    width = kv_weight.shape[0]
    pair = kv_weight.shape[1] * kv_weight.shape[2]
    clips = destination.shape[0] // rows
    slots = clips * CAPACITY
    tokens = queries.shape[0]
    blocks = width // feat
    half = rows // 2
    dma = pltpu.SemaphoreType.DMA
    return pl.pallas_call(
        kernel,
        out_shape=pltpu.VMEM(queries.shape, BF16),
        in_specs=[pl.BlockSpec(memory_space=pl.ANY)] * 7,
        out_specs=pl.BlockSpec(memory_space=pltpu.VMEM),
        scratch_shapes=[
            pltpu.VMEM((rows, hidden), BF16),
            pltpu.VMEM((hidden, feat), BF16),
            pltpu.VMEM((rows, feat), BF16),
            pltpu.VMEM((1, width), F32),
            pltpu.VMEM((2, width, pair), BF16),
            pltpu.VMEM((clips, rows), jnp.int32),
            pltpu.VMEM((slots, rows), BF16),
            pltpu.VMEM((1, slots), F32),
            pltpu.VMEM((rows, feat), F32),
            pltpu.VMEM((half, feat), F32),
            pltpu.VMEM((blocks, half, feat), BF16),
            pltpu.VMEM((half, width), BF16),
            pltpu.VMEM((half, pair), BF16),
            pltpu.VMEM((rows, pair), BF16),
            pltpu.VMEM((slots, pair), BF16),
            pltpu.VMEM((ZS, slots, pair), BF16),
            pltpu.VMEM((pair // 2, slots), BF16),
            pltpu.VMEM((ZS, 4 * tokens, 128), BF16),
            pltpu.VMEM((ZS, 4 * tokens, 128), BF16),
            dma((9 + 2 * (hidden // 1024),)),
            dma,
            dma,
            dma,
            dma,
            dma,
            dma((blocks,)),
            dma,
            dma((ZS,)),
            dma,
            dma,
            dma,
            dma((clips // XS,)),
            dma,
            dma((ZS * clips // XS,)),
            dma,
            dma,
        ],
        compiler_params=pltpu.CompilerParams(
            collective_id=0, has_side_effects=True, vmem_limit_bytes=56 * 1024 * 1024
        ),
    )(
        ffn_hidden,
        ffn_weight,
        residual,
        norm_gain.reshape(1, width),
        kv_weight.reshape(width, pair),
        destination.reshape(clips, rows),
        queries,
    )


def solution(mesh):
    return jax.shard_map(
        shards,
        mesh=mesh,
        in_specs=(
            P("clip", "tp"),
            P("tp", "seq"),
            P("clip", "seq"),
            P(),
            P(None, ("seq", "tp"), None),
            P(),
            P(("clip", "seq", "tp"), None),
        ),
        out_specs=P(("clip", "seq", "tp"), None),
        check_vma=False,
    )
```

```python
import math

import jax
import jax.numpy as jnp
from jax import lax
from jax.experimental import pallas as pl
from jax.experimental.pallas import tpu as pltpu
from jax.sharding import PartitionSpec as P

EPSILON = 1e-06
MESH = pl.DeviceIdType.MESH
F32 = jnp.float32
BF16 = jnp.bfloat16
CAPACITY = 16
AT_START, IN_GATHER = 1, 2
EARLY = 4
ZS = 8
XS = 8


def remote(src, dst, send_sem, recv_sem, device):
    return pltpu.make_async_remote_copy(
        src_ref=src,
        dst_ref=dst,
        send_sem=send_sem,
        recv_sem=recv_sem,
        device_id=device,
        device_id_type=MESH,
    )


def near_step(k):
    return (1 - 2 * (k % 2)) * ((k + 1) // 2)


def gray(i):
    return i + (i // 2) * (1 - 2 * (i % 2))


def kernel(
    hid,
    wt,
    res,
    gain,
    kvw,
    dest,
    qry,
    out,
    hid_v,
    wt_v,
    res_v,
    gain_v,
    w2_v,
    dest_v,
    sel_v,
    bias_v,
    part,
    part_in,
    tbuf,
    nbuf,
    kv_out,
    kv_rows,
    packed,
    kvall,
    kt_v,
    qbuf,
    rbuf,
    ld,
    tp_s,
    tp_r,
    w_s,
    w_r,
    ag_s,
    ag_r,
    q_s,
    q_r,
    kx_s,
    kx_r,
    c_s,
    c_r,
    k_s,
    k_r,
    r_s,
    r_r,
    ready,
):
    clips = lax.axis_size("clip")
    c, s, t = lax.axis_index("clip"), lax.axis_index("seq"), lax.axis_index("tp")
    y, z = s // ZS, s % ZS
    yh, x = c // XS, c % XS
    parts = clips // XS
    other = 1 - t
    partner = (c, s, other)
    across = (1 - y) * ZS + z
    member = 2 * y + t
    rows = hid_v.shape[0]
    half = rows // 2
    feat = part.shape[1]
    blocks = tbuf.shape[0]
    hd = 128
    chunk = XS * CAPACITY

    def column(j):
        return pl.ds(pl.multiple_of(j * hd, hd), hd)

    def block_rows(j, size):
        return pl.ds(pl.multiple_of(j * size, size), size)

    step = 1024
    depths = [pl.ds(k * step, step) for k in range(hid_v.shape[1] // step)]
    loads = []
    for k, at in enumerate(depths):
        loads.append(pltpu.make_async_copy(hid.at[:, at], hid_v.at[:, at], ld.at[9 + 2 * k]))
        loads.append(pltpu.make_async_copy(wt.at[at], wt_v.at[at], ld.at[10 + 2 * k]))
    dest_load = pltpu.make_async_copy(dest, dest_v, ld.at[0])
    res_load = pltpu.make_async_copy(res, res_v, ld.at[3])
    gain_load = pltpu.make_async_copy(gain, gain_v, ld.at[4])
    w_load = pltpu.make_async_copy(kvw, w2_v.at[t], ld.at[5])
    for load in loads:
        load.start()

    barrier = pltpu.get_barrier_semaphore()

    def greet(device):
        pl.semaphore_signal(barrier, inc=1, device_id=device, device_id_type=MESH)

    @pl.loop(1, parts)
    def _(o):
        greet(((yh + o) % parts * XS + x, s, t))

    @pl.loop(1, XS)
    def _(o):
        greet((yh * XS + (x + o) % XS, s, t))

    @pl.loop(1, ZS)
    def _(o):
        greet((c, y * ZS + (z + o) % ZS, t))

    for d in (-2, -1, 0, 1, 2):
        greet((c, (1 - y) * ZS + (z + d + ZS) % ZS, t))

    greet((c, across, other))
    greet(partner)

    for load in (res_load, dest_load, gain_load, w_load):
        load.start()

    @pl.loop(0, ZS)
    def _(k):
        pltpu.make_async_copy(
            qry.at[:, column(2 * (y * ZS + k) + t)],
            qbuf.at[k, block_rows(member, rows)],
            ld.at[6],
        ).start()

    total = jnp.zeros(part.shape, F32)
    for k, at in enumerate(depths):
        loads[2 * k].wait()
        loads[2 * k + 1].wait()
        total += jnp.dot(hid_v[:, at], wt_v[at, :], preferred_element_type=F32)
    part[...] = total

    pl.semaphore_wait(barrier, ZS - 1 + 7 + parts - 1 + XS - 1)

    @pl.loop(1, parts)
    def _(o):
        peer = ((yh + o) % parts * XS + x, s, t)
        pl.semaphore_signal(ready, inc=1, device_id=peer, device_id_type=MESH)

    tp_copy = remote(part.at[block_rows(other, half)], part_in, tp_s, tp_r, partner)
    tp_copy.start()
    res_load.wait()
    tp_copy.wait_recv()
    mine = part[block_rows(t, half), :] + part_in[...]
    text = res_v[block_rows(t, half), :].astype(F32) + mine
    tbuf[s] = text.astype(BF16)

    def text_copy(block, device):
        return remote(tbuf.at[block], tbuf.at[block], ag_s, ag_r.at[block], device)

    def along(d):
        return y * ZS + (z + d + ZS) % ZS

    def beside(d):
        return (1 - y) * ZS + (z + d + ZS) % ZS

    def pass_on(block, to):
        text_copy(block, (c, to, t)).start()

    for to in (across, along(-1), along(1), along(-2), along(2)):
        pass_on(s, to)

    def send_queries(k):
        at = (z + near_step(k) + ZS) % ZS
        for peer_y, peer_t in ((1 - y, t), (1 - y, other), (y, other)):
            remote(
                qry.at[:, column(2 * (peer_y * ZS + at) + peer_t)],
                qbuf.at[at, block_rows(member, rows)],
                q_s,
                q_r.at[at],
                (c, peer_y * ZS + z, peer_t),
            ).start()

    @pl.loop(0, AT_START)
    def _(k):
        send_queries(k)

    weights = remote(kvw, w2_v.at[t], w_s, w_r, partner)
    weights.start()

    dest_load.wait()
    dest_row = dest_v[pl.ds(c, 1), :]
    clip_ids = lax.broadcasted_iota(jnp.int32, (clips, rows), 0)
    onehot = jnp.where(clip_ids == dest_row, 1.0, 0.0)
    earlier = jnp.where(
        lax.broadcasted_iota(jnp.int32, (rows, rows), 0)
        < lax.broadcasted_iota(jnp.int32, (rows, rows), 1),
        1.0,
        0.0,
    ).astype(BF16)
    before = jnp.dot(onehot.astype(BF16), earlier, preferred_element_type=F32)
    rank = jnp.sum(before * onehot, axis=0, keepdims=True)
    place = dest_row * CAPACITY + rank.astype(jnp.int32)
    slots = clips * CAPACITY
    target = lax.broadcasted_iota(jnp.int32, (slots, rows), 0)
    sel_v[...] = jnp.where(target == place, 1.0, 0.0).astype(BF16)
    counts = jnp.sum(jnp.where(dest_v[...] == c, 1.0, 0.0), axis=1, keepdims=True)
    slot = lax.broadcasted_iota(jnp.int32, (clips, slots), 1)
    source = lax.broadcasted_iota(jnp.int32, (clips, slots), 0)
    in_block = jnp.where(slot // CAPACITY == source, counts, 0.0)
    filled = jnp.sum(in_block, axis=0, keepdims=True)
    position = (lax.broadcasted_iota(jnp.int32, (1, slots), 1) % CAPACITY).astype(F32)
    bias_v[...] = jnp.where(position < filled, 0.0, -1e30)

    for d in (-1, 1, -2, 2, -3, 3, 4):
        block = along(d)
        text_copy(block, (c, across, t)).wait_recv()
        if d in (-2, 2):
            onward = -d // 2
            pass_on(block, along(onward))
            pass_on(block, beside(onward))

            @pl.when(t == (0 if d < 0 else 1))
            def _(block=block, onward=onward):
                pass_on(block, along(2 * onward))
                pass_on(block, beside(2 * onward))

        if abs(d) < 3:
            pass_on(block, across)
        if d == 2:

            @pl.loop(AT_START, IN_GATHER)
            def _(k):
                send_queries(k)

    @pl.loop(0, ZS)
    def _(k):
        text_copy((1 - y) * ZS + k, (c, across, t)).wait_recv()

    @pl.loop(IN_GATHER, EARLY)
    def _(k):
        send_queries(k)

    gain_load.wait()

    def squares(b, acc):
        wide = tbuf[b].astype(F32)
        return acc + wide * wide

    total = lax.fori_loop(0, blocks, squares, jnp.zeros((half, feat), F32))
    mean = jnp.sum(total, axis=1, keepdims=True) / (blocks * feat)
    scale = lax.rsqrt(mean + EPSILON)

    @pl.loop(0, blocks)
    def _(b):
        at = pl.ds(pl.multiple_of(b * feat, feat), feat)
        nbuf[:, at] = (tbuf[b].astype(F32) * scale * gain_v[:, at]).astype(BF16)

    def project(head):
        acc = jnp.zeros((half, 2 * hd), F32)
        for k in range(blocks * feat // step):
            at = pl.ds(k * step, step)
            acc += jnp.dot(nbuf[:, at], w2_v[head, at, :], preferred_element_type=F32)
        return acc.astype(BF16)

    weights.wait_recv()
    kv_out[...] = project(other)
    swap = remote(kv_out, kv_rows.at[block_rows(t, half)], kx_s, kx_r, partner)
    swap.start()
    w_load.wait()
    kv_rows[block_rows(t, half), :] = project(t)
    remote(kv_out, kv_rows.at[block_rows(other, half)], kx_s, kx_r, partner).wait_recv()

    pl.semaphore_wait(ready, parts - 1)

    @pl.loop(0, parts)
    def _(i):
        to = (yh + gray(i)) % parts
        at = block_rows(to, chunk)
        packed[at, :] = jnp.dot(sel_v[at, :], kv_rows[...], preferred_element_type=F32).astype(BF16)

        @pl.loop(0, XS)
        def _(j):
            d = to * XS + (x + XS // 2 + j) % XS

            @pl.when(d != c)
            def _():
                remote(
                    packed.at[block_rows(d, CAPACITY)],
                    kvall.at[z, block_rows(c, CAPACITY)],
                    c_s,
                    c_r.at[i],
                    (d, s, t),
                ).start()

    stay = pltpu.make_async_copy(
        packed.at[block_rows(c, CAPACITY)], kvall.at[z, block_rows(c, CAPACITY)], ld.at[7]
    )
    stay.start()
    own_queries = pltpu.make_async_copy(qbuf.at[pl.ds(0, 2)], qbuf.at[pl.ds(0, 2)], ld.at[6])
    own_queries.wait()
    stay.wait()

    factor = 1.0 / math.sqrt(hd)
    up, down = (c, y * ZS + (z + 1) % ZS, t), (c, y * ZS + (z + ZS - 1) % ZS, t)

    def chunk_copy(place, i, device):
        at = block_rows((yh - gray(i) + parts) % parts, chunk)
        piece = kvall.at[place, at]
        return remote(piece, piece, k_s, k_r.at[place * parts + i], device)

    def arrived(i, size):
        piece = kvall.at[z, pl.ds(0, size)]
        remote(packed.at[pl.ds(0, size)], piece, c_s, c_r.at[i], partner).wait_recv()

    def unit_of(n):
        e, i = n // parts - 1, n % parts
        return (z + (2 * (i // 2) - 1) * e + ZS) % ZS, (i + 1 + y) % 2

    def result_copy(place, peer_y, peer_t):
        return remote(
            rbuf.at[place, block_rows(2 * peer_y + peer_t, rows)],
            out.at[:, column(2 * (y * ZS + place) + t)],
            r_s,
            r_r,
            (c, peer_y * ZS + z, peer_t),
        )

    def send_unit(n):
        place, peer_y = unit_of(n)

        @pl.when(peer_y == y)
        def _():
            result_copy(place, y, other).start()
            pltpu.make_async_copy(
                rbuf.at[place, block_rows(member, rows)],
                out.at[:, column(2 * (y * ZS + place) + t)],
                ld.at[8],
            ).start()

        @pl.when(peer_y != y)
        def _():
            result_copy(place, 1 - y, t).start()
            result_copy(place, 1 - y, other).start()

    def order_of(n):
        m, late = n % 8, (n // 8 + 1) // 2
        some, end = (m + 7) // 8, m // 7
        d = some * ((1 - m % 2) * (1 - end) + end)
        i = some * ((m % 2) * ((m + 1) // 2) + (1 - m % 2) * (m // 2 - 1)) - end
        return late * (n // parts) + (1 - late) * d, late * (n % parts) + (1 - late) * i

    first, last = 2 * parts - 2, parts * (ZS // 2 + 1) + 1

    @pl.loop(0, last + 1)
    def _(n):
        d, i = order_of(n)
        low, high = (z - d + ZS) % ZS, (z + d) % ZS

        @pl.when(n == 0)
        def _():
            arrived(i, chunk - CAPACITY)

        @pl.when((n > 0) & (d == 0))
        def _():
            arrived(i, chunk)

        @pl.when((d > 0) & (d < ZS // 2))
        def _():
            chunk_copy(low, i, up).wait_recv()

        @pl.when((d < 3) | ((d == 3) & (i < 2)))
        def _():
            chunk_copy(low, i, up).start()

        @pl.when((d > 0) & (d < ZS // 2))
        def _():
            chunk_copy(high, i, down).wait_recv()

        @pl.when((d < 3) | ((d == 3) & (i >= 2)))
        def _():
            chunk_copy(high, i, down).start()

        @pl.when((n >= 5) & (n < 5 + ZS - EARLY))
        def _():
            send_queries(n - 5 + EARLY)

        @pl.when(n > first)
        def _():
            send_unit(n - 1)

        @pl.when(n == last - 1)
        def _():
            @pl.loop(0, parts)
            def _(k):
                chunk_copy((z + ZS // 2) % ZS, k, up).wait_recv()

        @pl.when(n >= first)
        def _():
            place, peer_y = unit_of(n)

            @pl.when(i % 2 == 0)
            def _():
                into = qbuf.at[place, pl.ds(0, 3 * rows)]
                remote(into, into, q_s, q_r.at[place], partner).wait_recv()
                kt_v[...] = kvall[place, :, :hd].T

            tokens = block_rows(peer_y, 2 * rows)
            scores = jnp.dot(qbuf[place, tokens, :], kt_v[...], preferred_element_type=F32)
            scores = scores * factor + bias_v[...]
            peak = jnp.max(scores, axis=1, keepdims=True)
            w = jnp.exp(scores - peak)
            probs = (w * (1.0 / jnp.sum(w, axis=1, keepdims=True))).astype(BF16)
            attended = jnp.dot(probs, kvall[place, :, hd:], preferred_element_type=F32)
            rbuf[place, tokens, :] = attended.astype(BF16)

    tp_copy.wait_send()
    weights.wait_send()
    remote(tbuf.at[pl.ds(0, 2 * ZS - 1)], tbuf.at[pl.ds(0, 2 * ZS - 1)], ag_s, ag_r.at[s], partner).wait_send()
    swap.wait_send()
    remote(packed.at[pl.ds(0, slots - CAPACITY)], packed.at[pl.ds(0, slots - CAPACITY)], c_s, c_r.at[0], partner).wait_send()
    send_unit(last)
    most = pl.ds(0, 3 * ZS // 4)
    remote(qbuf.at[most], qbuf.at[most], q_s, q_r.at[0], partner).wait_send()
    remote(kvall.at[pl.ds(0, ZS - 1)], kvall.at[pl.ds(0, ZS - 1)], k_s, k_r.at[0], partner).wait_send()
    here = out.at[:, pl.ds(0, ZS * hd)]
    pltpu.make_async_copy(here, here, ld.at[8]).wait()
    results = remote(rbuf.at[most], out.at[:, pl.ds(0, 3 * ZS * hd)], r_s, r_r, partner)
    results.wait_send()
    results.wait_recv()


def shards(ffn_hidden, ffn_weight, residual, norm_gain, kv_weight, destination, queries):
    rows, hidden = ffn_hidden.shape
    feat = ffn_weight.shape[1]
    width = kv_weight.shape[0]
    pair = kv_weight.shape[1] * kv_weight.shape[2]
    clips = destination.shape[0] // rows
    slots = clips * CAPACITY
    tokens = queries.shape[0]
    blocks = width // feat
    half = rows // 2
    dma = pltpu.SemaphoreType.DMA
    return pl.pallas_call(
        kernel,
        out_shape=pltpu.VMEM(queries.shape, BF16),
        in_specs=[pl.BlockSpec(memory_space=pl.ANY)] * 7,
        out_specs=pl.BlockSpec(memory_space=pltpu.VMEM),
        scratch_shapes=[
            pltpu.VMEM((rows, hidden), BF16),
            pltpu.VMEM((hidden, feat), BF16),
            pltpu.VMEM((rows, feat), BF16),
            pltpu.VMEM((1, width), F32),
            pltpu.VMEM((2, width, pair), BF16),
            pltpu.VMEM((clips, rows), jnp.int32),
            pltpu.VMEM((slots, rows), BF16),
            pltpu.VMEM((1, slots), F32),
            pltpu.VMEM((rows, feat), F32),
            pltpu.VMEM((half, feat), F32),
            pltpu.VMEM((blocks, half, feat), BF16),
            pltpu.VMEM((half, width), BF16),
            pltpu.VMEM((half, pair), BF16),
            pltpu.VMEM((rows, pair), BF16),
            pltpu.VMEM((slots, pair), BF16),
            pltpu.VMEM((ZS, slots, pair), BF16),
            pltpu.VMEM((pair // 2, slots), BF16),
            pltpu.VMEM((ZS, 4 * tokens, 128), BF16),
            pltpu.VMEM((ZS, 4 * tokens, 128), BF16),
            dma((9 + 2 * (hidden // 1024),)),
            dma,
            dma,
            dma,
            dma,
            dma,
            dma((blocks,)),
            dma,
            dma((ZS,)),
            dma,
            dma,
            dma,
            dma((clips // XS,)),
            dma,
            dma((ZS * clips // XS,)),
            dma,
            dma,
            pltpu.SemaphoreType.REGULAR,
        ],
        compiler_params=pltpu.CompilerParams(
            collective_id=0, has_side_effects=True, vmem_limit_bytes=56 * 1024 * 1024
        ),
    )(
        ffn_hidden,
        ffn_weight,
        residual,
        norm_gain.reshape(1, width),
        kv_weight.reshape(width, pair),
        destination.reshape(clips, rows),
        queries,
    )


def solution(mesh):
    return jax.shard_map(
        shards,
        mesh=mesh,
        in_specs=(
            P("clip", "tp"),
            P("tp", "seq"),
            P("clip", "seq"),
            P(),
            P(None, ("seq", "tp"), None),
            P(),
            P(("clip", "seq", "tp"), None),
        ),
        out_specs=P(("clip", "seq", "tp"), None),
        check_vma=False,
    )
```
